32 devices in a mesh: head: 4 (over z), span: 8 (over y, x, core).
Axes of the slice: x: 2, y: 2, z: 4, core: 2. Of those that a mesh axis runs over, the one named last changes fastest.
Arguments:
- queries: bfloat16 [4096, 2048], P(('span', 'head')), may hold values from -6 to 6
- keys: bfloat16 [4096, 2048], P(('span', 'head')), may hold values from -6 to 6
- values: bfloat16 [4096, 2048], P(('span', 'head')), may hold values from -6 to 6
- out_grad: bfloat16 [4096, 2048], P(('span', 'head')), may hold values from -6 to 6
Outputs:
- attn_out: bfloat16 [4096, 2048], P(('span', 'head'))
- query_gradient: bfloat16 [4096, 2048], P(('span', 'head'))
- grad_key: bfloat16 [4096, 2048], P(('span', 'head'))
- grad_value: bfloat16 [4096, 2048], P(('span', 'head'))
The draws below stay inside these ranges and needn't reach their ends.
All inputs are finite; a program needn't handle non-finite values.
Results may differ from the reference program's by a relative error of at most 0.0058.
Values may be sent and summed in bfloat16 or wider, within the bound.
No kernel may reach another device: no remote copies, remote signals or barrier semaphores. Data moves between devices by JAX's collectives and lax.ppermute only.
A program may use at most 64 MiB of HBM per device.

```python
import jax
import jax.numpy as jnp
from jax import lax

HEADS = 16
DH = 128
BLK = 512
SEQ = 4096
FEAT = 2048


def levels(stream_key, shape, shards, smallest, top_value):
    level = 1.0
    for dim, shards_of in shards:
        heights = jax.random.uniform(jax.random.fold_in(jax.random.fold_in(stream_key, 6), dim), (shards_of,), jnp.float32, smallest / len(shards), top_value / len(shards))
        level = level * jnp.repeat(jnp.exp(heights), shape[dim] // shards_of).reshape((-1,) + (1,) * (len(shape) - 1 - dim))
    return level


def scatter_about(stream_key, extent, deviation, limit, cuts=(), kind=jnp.bfloat16):
    drawn = deviation * jax.random.normal(stream_key, extent, jnp.float32)
    if cuts:
        drawn = drawn * levels(stream_key, extent, cuts, -0.22, 0.18)
    return jnp.clip(drawn, -limit, limit).astype(kind)


def setup_inputs(seed: int = 0) -> dict:
    splits = jax.random.split(jax.random.key(seed), 5)
    return {
        "queries": scatter_about(splits[0], (SEQ, FEAT), 1.0, 6.0, ((0, 32),)),
        "keys": scatter_about(splits[1], (SEQ, FEAT), 1.0, 6.0, ((0, 32),)),
        "values": scatter_about(splits[2], (SEQ, FEAT), 1.0, 6.0, ((0, 32),)),
        "out_grad": scatter_about(splits[3], (SEQ, FEAT), 1.0, 6.0, ((0, 32),)),
    }


def block_states(items):
    key_tile, value_tile, query_block, scaled_block = items
    forward_every = jnp.einsum('xgy,xgi->gyi', key_tile.astype(jnp.float32), value_tile.astype(jnp.float32))
    back_each = jnp.einsum('tnv,tnk->nvk', scaled_block.astype(jnp.float32), query_block.astype(jnp.float32))
    return (forward_every, back_each)

def block_terms(items):
    query_block, key_tile, value_tile, scaled_block, forward_narrow, back_low, scale_block = items
    token_count = query_block.shape[0]
    causal = jnp.tril(jnp.ones((token_count, token_count), dtype=jnp.bool_))
    query_wide = query_block.astype(jnp.float32)
    key_wide = key_tile.astype(jnp.float32)
    value_float = value_tile.astype(jnp.float32)
    scaled_wide = scaled_block.astype(jnp.float32)
    forward_wide = forward_narrow.astype(jnp.float32)
    back_float = back_low.astype(jnp.float32)
    raw_scores = jnp.einsum('tnd,snd->nts', query_wide, key_wide)
    scores = jnp.where(causal[None], raw_scores, 0.0).astype(jnp.bfloat16)
    scores = lax.optimization_barrier(scores).astype(jnp.float32)
    raw_grads = jnp.einsum('tnd,snd->nts', scaled_wide, value_float)
    score_gradient = jnp.where(causal[None], raw_grads, 0.0).astype(jnp.bfloat16)
    score_gradient = lax.optimization_barrier(score_gradient).astype(jnp.float32)
    local_out = jnp.einsum('epa,aev->pev', scores, value_float)
    carried_result = jnp.einsum('rwb,wbo->rwo', query_wide, forward_wide)
    attn_out = ((local_out + carried_result) * scale_block[:, None, None]).astype(jnp.bfloat16)
    query_gradient = (jnp.einsum('epa,aev->pev', score_gradient, key_wide) + jnp.einsum('hsx,smx->hsm', scaled_wide, forward_wide)).astype(jnp.bfloat16)
    grad_key = (jnp.einsum('nts,tnd->snd', score_gradient, query_wide) + jnp.einsum('snv,nvk->snk', value_float, back_float)).astype(jnp.bfloat16)
    grad_value = (jnp.einsum('nts,tnd->snd', scores, scaled_wide) + jnp.einsum('snk,nvk->snv', key_wide, back_float)).astype(jnp.bfloat16)
    return (attn_out, query_gradient, grad_key, grad_value)

def reference(queries, keys, values, out_grad):
    block_count = SEQ // BLK
    block_shape = (block_count, BLK, HEADS, DH)
    position = jnp.arange(SEQ, dtype=jnp.int32)
    position_scale = 1.0 / jnp.sqrt(jnp.float32(DH) * (position + 1).astype(jnp.float32))
    scaled = (out_grad.astype(jnp.float32) * position_scale[:, None]).astype(jnp.bfloat16)
    scaled = lax.optimization_barrier(scaled)
    query_blocks = queries.reshape(block_shape)
    key_blocks = keys.reshape(block_shape)
    value_blocks = values.reshape(block_shape)
    scaled_blocks = scaled.reshape(block_shape)
    scale_blocks = position_scale.reshape(block_count, BLK)
    forward_every, back_each = lax.map(block_states, (key_blocks, value_blocks, query_blocks, scaled_blocks))
    fwd_state = jnp.cumsum(forward_every, axis=0) - forward_every
    back_state = lax.optimization_barrier(jnp.sum(back_each, axis=0))[None] - jnp.cumsum(back_each, axis=0)
    forward_narrow = lax.optimization_barrier(fwd_state.astype(jnp.bfloat16))
    back_low = lax.optimization_barrier(back_state.astype(jnp.bfloat16))
    outputs = lax.map(block_terms, (query_blocks, key_blocks, value_blocks, scaled_blocks, forward_narrow, back_low, scale_blocks))
    attn_out = outputs[0].reshape(SEQ, HEADS * DH)
    query_gradient = outputs[1].reshape(SEQ, HEADS * DH)
    grad_key = outputs[2].reshape(SEQ, HEADS * DH)
    grad_value = outputs[3].reshape(SEQ, HEADS * DH)
    return (attn_out, query_gradient, grad_key, grad_value)
```

```python
import functools

import jax
import jax.numpy as jnp
from jax import lax
from jax.experimental import pallas as pl
from jax.experimental.pallas import tpu as pltpu
from jax.sharding import PartitionSpec as P

HEADS = 16
DH = 128
STEP = 4
F32 = jnp.float32
BF16 = jnp.bfloat16
NT = (((1,), (1,)), ((), ()))
TN = (((0,), (0,)), ((), ()))


def dot(a, b, dims=None):
    if dims is None:
        return jnp.dot(a, b, preferred_element_type=F32)
    return lax.dot_general(a, b, dims, preferred_element_type=F32)


def coef_of(base, length):
    position = base + lax.broadcasted_iota(jnp.int32, (length, DH), 0)
    return 1.0 / jnp.sqrt(jnp.float32(DH) * (position + 1).astype(F32))


def states_kernel(base, q_ref, k_ref, v_ref, g_ref, st_ref, scaled_ref):
    coef = coef_of(base[0], q_ref.shape[0])
    parts = DH // st_ref.shape[2]
    for h in range(STEP):
        cols = pl.ds(h * DH, DH)
        scaled = (g_ref[:, cols].astype(F32) * coef).astype(BF16)
        scaled_ref[:, cols] = scaled
        fwd = dot(k_ref[:, cols], v_ref[:, cols], TN).astype(BF16)
        back = dot(scaled, q_ref[:, cols], TN).astype(BF16)
        rows = pl.ds(h * parts, parts)
        st_ref[rows, 0] = fwd.reshape(parts, DH // parts, DH)
        st_ref[rows, 1] = back.reshape(parts, DH // parts, DH)


def scores_kernel(q_ref, k_ref, v_ref, c_ref, sc_ref, sct_ref, ds_ref, dst_ref):
    length = q_ref.shape[0]
    row = lax.broadcasted_iota(jnp.int32, (length, length), 0)
    col = lax.broadcasted_iota(jnp.int32, (length, length), 1)
    lower, upper = col <= row, col >= row
    for h in range(STEP):
        cols = pl.ds(h * DH, DH)
        q, k, v, c = q_ref[:, cols], k_ref[:, cols], v_ref[:, cols], c_ref[:, cols]
        sc_ref[h] = jnp.where(lower, dot(q, k, NT), 0.0).astype(BF16)
        sct_ref[h] = jnp.where(upper, dot(k, q, NT), 0.0).astype(BF16)
        ds_ref[h] = jnp.where(lower, dot(c, v, NT), 0.0).astype(BF16)
        dst_ref[h] = jnp.where(upper, dot(v, c, NT), 0.0).astype(BF16)


def scan_kernel(in_ref, out_ref):
    count = in_ref.shape[0]
    shape = in_ref.shape[2:]

    def step(i, carry):
        fwd, back = carry
        out_ref[i, 0] = fwd.astype(BF16)
        last = count - 1 - i
        out_ref[last, 1] = back.astype(BF16)
        return fwd + in_ref[i, 0].astype(F32), back + in_ref[last, 1].astype(F32)

    lax.fori_loop(0, count, step, (jnp.zeros(shape, F32), jnp.zeros(shape, F32)))


def final_kernel(
    base, q_ref, k_ref, v_ref, c_ref, sc_ref, sct_ref, ds_ref, dst_ref, fb_ref,
    out_ref, dq_ref, dk_ref, dv_ref,
):
    coef = coef_of(base[0], q_ref.shape[0])
    parts = DH // fb_ref.shape[2]
    for h in range(STEP):
        cols = pl.ds(h * DH, DH)
        q, k, v, c = q_ref[:, cols], k_ref[:, cols], v_ref[:, cols], c_ref[:, cols]
        rows = pl.ds(h * parts, parts)
        fwd = fb_ref[rows, 0].reshape(DH, DH)
        back = fb_ref[rows, 1].reshape(DH, DH)
        out_ref[:, cols] = ((dot(sc_ref[h], v) + dot(q, fwd)) * coef).astype(BF16)
        dq_ref[:, cols] = (dot(ds_ref[h], k) + dot(c, fwd, NT)).astype(BF16)
        dk_ref[:, cols] = (dot(dst_ref[h], q) + dot(v, back)).astype(BF16)
        dv_ref[:, cols] = (dot(sct_ref[h], c) + dot(k, back, NT)).astype(BF16)


def shards(queries, keys, values, out_grad):
    axes = ("span", "head")
    devices = lax.axis_size(axes)
    length, feat = queries.shape
    base = (lax.axis_index(axes) * length).astype(jnp.int32).reshape(1)
    share = feat // devices
    direct = share % 16 == 0
    block = share if direct else DH
    count = feat // block
    grid = (HEADS // STEP,)
    tokens = pl.BlockSpec((length, STEP * DH), lambda i: (0, i))
    scalar = pl.BlockSpec(memory_space=pltpu.SMEM)
    state = pl.BlockSpec((STEP * DH // block, 2, block, DH), lambda i: (i, 0, 0, 0))
    square = pl.BlockSpec((STEP, length, length), lambda i: (i, 0, 0))
    rows_of = jax.ShapeDtypeStruct((length, feat), BF16)
    square_of = jax.ShapeDtypeStruct((HEADS, length, length), BF16)
    state_of = jax.ShapeDtypeStruct((count, 2, block, DH), BF16)

    states, scaled = pl.pallas_call(
        states_kernel,
        grid=grid,
        in_specs=[scalar] + [tokens] * 4,
        out_specs=[state, tokens],
        out_shape=[state_of, rows_of],
        name="states",
    )(base, queries, keys, values, out_grad)
    squares = pl.pallas_call(
        scores_kernel,
        grid=grid,
        in_specs=[tokens] * 4,
        out_specs=[square] * 4,
        out_shape=[square_of] * 4,
        name="scores",
    )(queries, keys, values, scaled)

    if direct:
        gathered = lax.all_to_all(states, axes, split_axis=0, concat_axis=0, tiled=True)
        summed = pl.pallas_call(
            scan_kernel, out_shape=jax.ShapeDtypeStruct(gathered.shape, BF16), name="scan"
        )(gathered)
        carried = lax.all_to_all(summed, axes, split_axis=0, concat_axis=0, tiled=True)
    else:
        cut = states.swapaxes(1, 2).reshape(devices, share, 2, DH)
        gathered = lax.all_to_all(cut, axes, split_axis=0, concat_axis=0, tiled=True)
        wide = gathered.astype(F32)
        fwd = jnp.cumsum(wide[:, :, 0], axis=0) - wide[:, :, 0]
        back = jnp.flip(jnp.cumsum(jnp.flip(wide[:, :, 1], 0), axis=0), 0) - wide[:, :, 1]
        summed = jnp.stack((fwd, back), axis=2).astype(BF16)
        carried = lax.all_to_all(summed, axes, split_axis=0, concat_axis=0, tiled=True)
        carried = carried.reshape(count, block, 2, DH).swapaxes(1, 2)

    return pl.pallas_call(
        final_kernel,
        grid=grid,
        in_specs=[scalar] + [tokens] * 4 + [square] * 4 + [state],
        out_specs=[tokens] * 4,
        out_shape=[rows_of] * 4,
        name="final",
    )(base, queries, keys, values, scaled, *squares, carried)


def solution(mesh):
    spec = P(("span", "head"), None)
    return jax.shard_map(
        shards, mesh=mesh, in_specs=(spec,) * 4, out_specs=(spec,) * 4, check_vma=False
    )
```

```python
import jax
import jax.numpy as jnp
from jax import lax
from jax.experimental import pallas as pl
from jax.experimental.pallas import tpu as pltpu
from jax.sharding import PartitionSpec as P


HEADS = 16
DH = 128
F32 = jnp.float32
BF16 = jnp.bfloat16
NT = (((1,), (1,)), ((), ()))
TN = (((0,), (0,)), ((), ()))
AXES = ("span", "head")
VMEM = 20 * 2**20


def dot(a, b, dims=None):
    if dims is None:
        return jnp.dot(a, b, preferred_element_type=F32)
    return lax.dot_general(a, b, dims, preferred_element_type=F32)


def coef_of(length):
    base = lax.axis_index(AXES) * length
    position = base + lax.broadcasted_iota(jnp.int32, (length, DH), 0)
    return 1.0 / jnp.sqrt(jnp.float32(DH) * (position + 1).astype(F32))


def group_of(k, groups):
    return lax.axis_index("head") ^ k if groups > 1 else 0


def columns(k, groups, h):
    first = (group_of(k, groups) * (HEADS // groups) + h) * DH
    return pl.ds(pl.multiple_of(first, DH), DH)


def fwd_states_kernel(k_ref, v_ref, s_ref):
    parts = DH // s_ref.shape[1]
    for h in range(HEADS):
        cols = pl.ds(h * DH, DH)
        fwd = dot(k_ref[:, cols], v_ref[:, cols], TN).astype(BF16)
        s_ref[pl.ds(h * parts, parts)] = fwd.reshape(parts, DH // parts, DH)


def back_states_kernel(q_ref, g_ref, c_ref, *t_refs):
    coef = coef_of(q_ref.shape[0])
    groups = len(t_refs)
    for k in reversed(range(groups)):
        for h in range(HEADS // groups):
            cols = columns(k, groups, h)
            scaled = (g_ref[:, cols].astype(F32) * coef).astype(BF16)
            c_ref[:, cols] = scaled
            t_refs[k][pl.ds(h * DH, DH), :] = dot(scaled, q_ref[:, cols], TN).astype(BF16)


def scores_kernel(q_ref, k_ref, v_ref, c_ref, sc_ref, sct_ref, ds_ref, dst_ref):
    length = q_ref.shape[0]
    row = lax.broadcasted_iota(jnp.int32, (length, length), 0)
    col = lax.broadcasted_iota(jnp.int32, (length, length), 1)
    lower, upper = col <= row, col >= row
    for h in range(HEADS):
        cols = pl.ds(h * DH, DH)
        q, k, v, c = q_ref[:, cols], k_ref[:, cols], v_ref[:, cols], c_ref[:, cols]
        sc_ref[h] = jnp.where(lower, dot(q, k, NT), 0.0).astype(BF16)
        sct_ref[h] = jnp.where(upper, dot(k, q, NT), 0.0).astype(BF16)
        ds_ref[h] = jnp.where(lower, dot(c, v, NT), 0.0).astype(BF16)
        dst_ref[h] = jnp.where(upper, dot(v, c, NT), 0.0).astype(BF16)


def fwd_scan_kernel(in_ref, out_ref):
    def step(i, total):
        out_ref[i] = total.astype(BF16)
        return total + in_ref[i].astype(F32)

    lax.fori_loop(0, in_ref.shape[0], step, jnp.zeros(in_ref.shape[1:], F32), unroll=4)


def total_kernel(*refs):
    total = refs[0][...].astype(F32)
    for ref in refs[1:-1]:
        total += ref[...].astype(F32)
    refs[-1][...] = total.astype(BF16)


def pair_kernel(a_ref, b_ref, out_ref):
    out_ref[...] = (a_ref[...].astype(F32) + b_ref[...].astype(F32)).astype(BF16)


def back_combine_kernel(groups, pair_ref, *refs):
    chips = len(refs) - 2 * groups - 1
    t_refs, chip_refs = refs[:groups], refs[groups : groups + chips]
    b_refs, held = refs[groups + chips : -1], refs[-1]
    span, plane = lax.axis_index("span"), lax.axis_index("head")
    for k in range(groups):
        held[plane ^ k] = t_refs[k][...]
    total = jnp.where(span % 2 == 0, pair_ref[...].astype(F32), 0.0)
    chip = span // 2
    for k in range(chips):
        after = (chip ^ (k + 1)) > chip
        total += jnp.where(after, chip_refs[k][...].astype(F32), 0.0)
    for z in reversed(range(groups)):
        own = held[z].astype(F32)
        held[z] = total.astype(BF16)
        total += own
    for k in range(groups):
        b_refs[k][...] = held[plane ^ k]


def fwd_final_kernel(q_ref, k_ref, v_ref, c_ref, sc_ref, ds_ref, f_ref, out_ref, dq_ref):
    coef = coef_of(q_ref.shape[0])
    parts = DH // f_ref.shape[1]
    for h in range(HEADS):
        cols = pl.ds(h * DH, DH)
        fwd = f_ref[pl.ds(h * parts, parts)].reshape(DH, DH)
        own = dot(sc_ref[h], v_ref[:, cols]) + dot(q_ref[:, cols], fwd)
        out_ref[:, cols] = (own * coef).astype(BF16)
        dq = dot(ds_ref[h], k_ref[:, cols]) + dot(c_ref[:, cols], fwd, NT)
        dq_ref[:, cols] = dq.astype(BF16)


def back_final_kernel(q_ref, k_ref, v_ref, c_ref, sct_ref, dst_ref, *refs):
    b_refs, dk_ref, dv_ref = refs[:-2], refs[-2], refs[-1]
    groups = len(b_refs)
    for k in range(groups):
        for h in range(HEADS // groups):
            cols = columns(k, groups, h)
            head = group_of(k, groups) * (HEADS // groups) + h
            back = b_refs[k][pl.ds(h * DH, DH), :]
            dk = dot(dst_ref[head], q_ref[:, cols]) + dot(v_ref[:, cols], back)
            dk_ref[:, cols] = dk.astype(BF16)
            dv = dot(sct_ref[head], c_ref[:, cols]) + dot(k_ref[:, cols], back, NT)
            dv_ref[:, cols] = dv.astype(BF16)


def exchange(x):
    return lax.all_to_all(x, AXES, split_axis=0, concat_axis=0, tiled=True)


def swap(x, axis, k):
    return lax.ppermute(x, axis, [(i, i ^ k) for i in range(lax.axis_size(axis))])


def call(kernel, out, flops, *args, scratch=()):
    moved = sum(a.size * a.dtype.itemsize for a in args)
    return pl.pallas_call(
        kernel,
        out_shape=out,
        scratch_shapes=list(scratch),
        cost_estimate=pl.CostEstimate(flops=flops, bytes_accessed=2 * moved, transcendentals=0),
        compiler_params=pltpu.CompilerParams(vmem_limit_bytes=VMEM),
    )(*args)


def shards(queries, keys, values, out_grad):
    devices, planes, span = lax.axis_size(AXES), lax.axis_size("head"), lax.axis_size("span")
    length, feat = queries.shape
    share = feat // devices
    direct = direct_on(devices, planes, span)
    block = share if direct else DH
    groups = planes if direct else 1
    rows_of = jax.ShapeDtypeStruct((length, feat), BF16)
    square_of = jax.ShapeDtypeStruct((HEADS, length, length), BF16)
    state_of = jax.ShapeDtypeStruct((feat // block, block, DH), BF16)
    piece_of = jax.ShapeDtypeStruct((feat // groups, DH), BF16)
    matmul = 2 * HEADS * length * DH * DH

    scaled, *back_states = call(
        back_states_kernel, [rows_of] + [piece_of] * groups, matmul,
        queries, out_grad,
    )
    if direct:
        own = [back_states[0]] + [swap(back_states[k], "head", k) for k in range(1, groups)]
    states = call(fwd_states_kernel, state_of, matmul, keys, values)
    if direct:
        gathered = exchange(states)
        fwd = exchange(
            call(fwd_scan_kernel, jax.ShapeDtypeStruct(gathered.shape, BF16), 0, gathered),
        )
        total = call(total_kernel, piece_of, 0, *own)
        other = swap(total, "span", 1)
        chip = call(pair_kernel, piece_of, 0, total, other)
        chips = [swap(chip, "span", 2 * k) for k in range(1, span // 2)]
        carried = call(
            lambda *refs: back_combine_kernel(groups, *refs),
            [piece_of] * groups, 0, other, *own, *chips,
            scratch=[pltpu.VMEM((groups, feat // groups, DH), BF16)],
        )
        back = [carried[0]] + [swap(carried[k], "head", k) for k in range(1, groups)]
    else:
        wide = exchange(states.reshape(devices, share, DH)).astype(F32)
        before = jnp.cumsum(wide, axis=0) - wide
        fwd = exchange(before.astype(BF16)).reshape(states.shape)
        wide = jnp.flip(exchange(back_states[0].reshape(devices, share, DH)), 0).astype(F32)
        after = jnp.flip(jnp.cumsum(wide, axis=0) - wide, 0)
        back = [exchange(after.astype(BF16)).reshape(feat, DH)]

    rows = (queries, keys, values, scaled)
    sc, sct, ds, dst = call(scores_kernel, [square_of] * 4, 4 * matmul, *rows)
    dk, dv = call(back_final_kernel, [rows_of] * 2, 4 * matmul, *rows, sct, dst, *back)
    out, dq = call(fwd_final_kernel, [rows_of] * 2, 4 * matmul, *rows, sc, ds, fwd)
    return out, dq, dk, dv


def direct_on(devices, planes, span):
    return HEADS * DH // devices % 16 == 0 and planes in (2, 4) and span in (2, 4, 8)


def solution(mesh):
    spec = P(AXES, None)

    return jax.shard_map(
        shards, mesh=mesh, in_specs=(spec,) * 4, out_specs=(spec,) * 4, check_vma=False
    )
```

```python
import jax
import jax.numpy as jnp
from jax import lax
from jax.experimental import pallas as pl
from jax.experimental.pallas import tpu as pltpu
from jax.sharding import PartitionSpec as P


HEADS = 16
DH = 128
F32 = jnp.float32
BF16 = jnp.bfloat16
NT = (((1,), (1,)), ((), ()))
TN = (((0,), (0,)), ((), ()))
AXES = ("span", "head")
VMEM = 20 * 2**20


def dot(a, b, dims=None):
    if dims is None:
        return jnp.dot(a, b, preferred_element_type=F32)
    return lax.dot_general(a, b, dims, preferred_element_type=F32)


def coef_of(length):
    base = lax.axis_index(AXES) * length
    position = base + lax.broadcasted_iota(jnp.int32, (length, DH), 0)
    return 1.0 / jnp.sqrt(jnp.float32(DH) * (position + 1).astype(F32))


def group_of(k, groups):
    return lax.axis_index("head") ^ k if groups > 1 else 0


def columns(k, groups, h):
    first = (group_of(k, groups) * (HEADS // groups) + h) * DH
    return pl.ds(pl.multiple_of(first, DH), DH)


def fwd_states_kernel(k_ref, v_ref, s_ref):
    parts = DH // s_ref.shape[1]
    for h in range(HEADS):
        cols = pl.ds(h * DH, DH)
        fwd = dot(k_ref[:, cols], v_ref[:, cols], TN).astype(BF16)
        s_ref[pl.ds(h * parts, parts)] = fwd.reshape(parts, DH // parts, DH)


def back_states_kernel(q_hbm, g_hbm, c_hbm, *refs):
    t_hbms, (q_ref, g_ref, c_ref, t_ref, in_sems, out_sems) = refs[:-6], refs[-6:]
    groups = len(t_hbms)
    width = HEADS // groups * DH
    order = list(range(1, groups)) + [0]
    loads = {}
    for k in order:
        cols = pl.ds(pl.multiple_of(group_of(k, groups) * width, DH), width)
        loads[k] = [
            pltpu.make_async_copy(g_hbm.at[:, cols], g_ref.at[k], in_sems.at[0, k]),
            pltpu.make_async_copy(q_hbm.at[:, cols], q_ref.at[k], in_sems.at[1, k]),
        ]
        for copy in loads[k]:
            copy.start()
    coef = coef_of(q_hbm.shape[0])
    stores = []
    for k in order:
        for copy in loads[k]:
            copy.wait()
        for h in range(HEADS // groups):
            cols = pl.ds(h * DH, DH)
            scaled = (g_ref[k, :, cols].astype(F32) * coef).astype(BF16)
            c_ref[k, :, cols] = scaled
            t_ref[k, cols, :] = dot(scaled, q_ref[k, :, cols], TN).astype(BF16)
        cols = pl.ds(pl.multiple_of(group_of(k, groups) * width, DH), width)
        group = [
            pltpu.make_async_copy(t_ref.at[k], t_hbms[k], out_sems.at[0, k]),
            pltpu.make_async_copy(c_ref.at[k], c_hbm.at[:, cols], out_sems.at[1, k]),
        ]
        for copy in group:
            copy.start()
        stores += group
    for copy in stores:
        copy.wait()


def fwd_scan_kernel(in_ref, out_ref):
    def step(i, total):
        out_ref[i] = total.astype(BF16)
        return total + in_ref[i].astype(F32)

    lax.fori_loop(0, in_ref.shape[0], step, jnp.zeros(in_ref.shape[1:], F32), unroll=4)


def total_kernel(*refs):
    total = refs[0][...].astype(F32)
    for ref in refs[1:-1]:
        total += ref[...].astype(F32)
    refs[-1][...] = total.astype(BF16)


def pair_kernel(a_ref, b_ref, out_ref):
    out_ref[...] = (a_ref[...].astype(F32) + b_ref[...].astype(F32)).astype(BF16)


def back_combine_kernel(groups, pair_ref, *refs):
    chips = len(refs) - 2 * groups - 1
    t_refs, chip_refs = refs[:groups], refs[groups : groups + chips]
    b_refs, held = refs[groups + chips : -1], refs[-1]
    span, plane = lax.axis_index("span"), lax.axis_index("head")
    for k in range(groups):
        held[plane ^ k] = t_refs[k][...]
    total = jnp.where(span % 2 == 0, pair_ref[...].astype(F32), 0.0)
    chip = span // 2
    for k in range(chips):
        after = (chip ^ (k + 1)) > chip
        total += jnp.where(after, chip_refs[k][...].astype(F32), 0.0)
    for z in reversed(range(groups)):
        own = held[z].astype(F32)
        held[z] = total.astype(BF16)
        total += own
    for k in range(groups):
        b_refs[k][...] = held[plane ^ k]


def masked(a, b, mask):
    return jnp.where(mask, dot(a, b, NT), 0.0).astype(BF16)


def square_of(length):
    row = lax.broadcasted_iota(jnp.int32, (length, length), 0)
    return row, lax.broadcasted_iota(jnp.int32, (length, length), 1)


def write(outs, held, sems, slot, first, width):
    cols = pl.ds(pl.multiple_of(first, DH), width)
    copies = [
        pltpu.make_async_copy(held.at[i, slot], out.at[:, cols], sems.at[i, slot])
        for i, out in enumerate(outs)
    ]
    for copy in copies:
        copy.start()
    return copies


def fwd_final_kernel(q_ref, k_ref, v_ref, c_ref, f_ref, out_hbm, dq_hbm, held, sems):
    length = q_ref.shape[0]
    coef = coef_of(length)
    parts = DH // f_ref.shape[1]
    slots = held.shape[1]
    row, col = square_of(length)
    copies = []
    for slot in range(slots):
        for i in range(HEADS // slots):
            h = slot * (HEADS // slots) + i
            cols, to = pl.ds(h * DH, DH), pl.ds(i * DH, DH)
            q, k, v, c = q_ref[:, cols], k_ref[:, cols], v_ref[:, cols], c_ref[:, cols]
            fwd = f_ref[pl.ds(h * parts, parts)].reshape(DH, DH)
            own = dot(masked(q, k, col <= row), v) + dot(q, fwd)
            held[0, slot, :, to] = (own * coef).astype(BF16)
            dq = dot(masked(c, v, col <= row), k) + dot(c, fwd, NT)
            held[1, slot, :, to] = dq.astype(BF16)
        width = HEADS // slots * DH
        copies += write((out_hbm, dq_hbm), held, sems, slot, slot * width, width)
    for copy in copies:
        copy.wait()


def back_final_kernel(q_ref, k_ref, v_ref, c_ref, *refs):
    b_refs, (dk_hbm, dv_hbm, held, sems) = refs[:-4], refs[-4:]
    groups = len(b_refs)
    slots = held.shape[1]
    row, col = square_of(q_ref.shape[0])
    copies = []
    for slot in range(slots):
        for i in range(HEADS // slots):
            g = slot * groups // slots
            h = slot * (HEADS // slots) + i - g * (HEADS // groups)
            cols, to = columns(g, groups, h), pl.ds(i * DH, DH)
            q, k, v, c = q_ref[:, cols], k_ref[:, cols], v_ref[:, cols], c_ref[:, cols]
            back = b_refs[g][pl.ds(h * DH, DH), :]
            dk = dot(masked(v, c, col >= row), q) + dot(v, back)
            held[0, slot, :, to] = dk.astype(BF16)
            dv = dot(masked(k, q, col >= row), c) + dot(k, back, NT)
            held[1, slot, :, to] = dv.astype(BF16)
        width = HEADS // slots * DH
        first = group_of(slot, groups) * width if groups > 1 else slot * width
        copies += write((dk_hbm, dv_hbm), held, sems, slot, first, width)
    for copy in copies:
        copy.wait()


def exchange(x):
    return lax.all_to_all(x, AXES, split_axis=0, concat_axis=0, tiled=True)


def swap(x, axis, k):
    return lax.ppermute(x, axis, [(i, i ^ k) for i in range(lax.axis_size(axis))])


def call(kernel, out, flops, *args, scratch=(), ins=None, outs=None, limit=VMEM):
    moved = sum(a.size * a.dtype.itemsize for a in args)
    vmem = pl.BlockSpec(memory_space=pltpu.VMEM)
    ins = [vmem] * len(args) if ins is None else ins
    if outs is None:
        outs = [vmem] * len(out) if isinstance(out, list) else vmem
    return pl.pallas_call(
        kernel,
        out_shape=out,
        in_specs=ins,
        out_specs=outs,
        scratch_shapes=list(scratch),
        cost_estimate=pl.CostEstimate(flops=flops, bytes_accessed=2 * moved, transcendentals=0),
        compiler_params=pltpu.CompilerParams(vmem_limit_bytes=limit),
    )(*args)


def shards(queries, keys, values, out_grad):
    devices, planes, span = lax.axis_size(AXES), lax.axis_size("head"), lax.axis_size("span")
    length, feat = queries.shape
    share = feat // devices
    direct = direct_on(devices, planes, span)
    block = share if direct else DH
    groups = planes if direct else 1
    rows_of = jax.ShapeDtypeStruct((length, feat), BF16)
    state_of = jax.ShapeDtypeStruct((feat // block, block, DH), BF16)
    piece_of = jax.ShapeDtypeStruct((feat // groups, DH), BF16)
    matmul = 2 * HEADS * length * DH * DH
    hbm = pl.BlockSpec(memory_space=pltpu.HBM)
    vmem = pl.BlockSpec(memory_space=pltpu.VMEM)
    staged = [pltpu.VMEM((groups, length, feat // groups), BF16)] * 3
    staged += [
        pltpu.VMEM((groups, feat // groups, DH), BF16),
        pltpu.SemaphoreType.DMA((2, groups)),
        pltpu.SemaphoreType.DMA((2, groups)),
    ]
    held = [
        pltpu.VMEM((2, 4, length, feat // 4), BF16),
        pltpu.SemaphoreType.DMA((2, 4)),
    ]

    scaled, *back_states = call(
        back_states_kernel, [rows_of] + [piece_of] * groups, matmul,
        queries, out_grad, scratch=staged, ins=[hbm] * 2, outs=[hbm] * (groups + 1), limit=None,
    )
    if direct:
        own = [back_states[0]] + [swap(back_states[k], "head", k) for k in range(1, groups)]
    states = call(fwd_states_kernel, state_of, matmul, keys, values)
    if direct:
        gathered = exchange(states)
        fwd = exchange(
            call(fwd_scan_kernel, jax.ShapeDtypeStruct(gathered.shape, BF16), 0, gathered),
        )
        total = call(total_kernel, piece_of, 0, *own)
        other = swap(total, "span", 1)
        chip = call(pair_kernel, piece_of, 0, total, other)
        chips = [swap(chip, "span", 2 * k) for k in range(1, span // 2)]
        carried = call(
            lambda *refs: back_combine_kernel(groups, *refs),
            [piece_of] * groups, 0, other, *own, *chips,
            scratch=[pltpu.VMEM((groups, feat // groups, DH), BF16)],
        )
        back = [carried[0]] + [swap(carried[k], "head", k) for k in range(1, groups)]
    else:
        wide = exchange(states.reshape(devices, share, DH)).astype(F32)
        before = jnp.cumsum(wide, axis=0) - wide
        fwd = exchange(before.astype(BF16)).reshape(states.shape)
        wide = jnp.flip(exchange(back_states[0].reshape(devices, share, DH)), 0).astype(F32)
        after = jnp.flip(jnp.cumsum(wide, axis=0) - wide, 0)
        back = [exchange(after.astype(BF16)).reshape(feat, DH)]

    rows = (queries, keys, values, scaled)
    out, dq = call(
        fwd_final_kernel, [rows_of] * 2, 6 * matmul, *rows, fwd,
        scratch=held, outs=[hbm] * 2,
    )
    dk, dv = call(
        back_final_kernel, [rows_of] * 2, 6 * matmul, *rows, *back,
        scratch=held, outs=[hbm] * 2,
    )
    return out, dq, dk, dv


def direct_on(devices, planes, span):
    return HEADS * DH // devices % 16 == 0 and planes in (2, 4) and span in (2, 4, 8)


def solution(mesh):
    spec = P(AXES, None)

    return jax.shard_map(
        shards, mesh=mesh, in_specs=(spec,) * 4, out_specs=(spec,) * 4, check_vma=False
    )
```

```python
import jax
import jax.numpy as jnp
from jax import lax
from jax.experimental import pallas as pl
from jax.experimental.pallas import tpu as pltpu
from jax.sharding import PartitionSpec as P


HEADS = 16
DH = 128
F32 = jnp.float32
BF16 = jnp.bfloat16
NT = (((1,), (1,)), ((), ()))
TN = (((0,), (0,)), ((), ()))
AXES = ("span", "head")
VMEM = 20 * 2**20


def dot(a, b, dims=None):
    if dims is None:
        return jnp.dot(a, b, preferred_element_type=F32)
    return lax.dot_general(a, b, dims, preferred_element_type=F32)


def coef_of(length):
    base = lax.axis_index(AXES) * length
    position = base + lax.broadcasted_iota(jnp.int32, (length, DH), 0)
    return 1.0 / jnp.sqrt(jnp.float32(DH) * (position + 1).astype(F32))


def group_of(k, groups):
    return lax.axis_index("head") ^ k if groups > 1 else 0


def columns(k, groups, h):
    first = (group_of(k, groups) * (HEADS // groups) + h) * DH
    return pl.ds(pl.multiple_of(first, DH), DH)


def fwd_states_kernel(k_ref, v_ref, s_ref):
    width = s_ref.shape[1] // DH
    for h in range(HEADS):
        cols = pl.ds(h * DH, DH)
        fwd = dot(k_ref[:, cols], v_ref[:, cols], TN).astype(BF16)
        s_ref[h // width, pl.ds(h % width * DH, DH), :] = fwd


def back_states_kernel(q_hbm, g_hbm, c_hbm, *refs):
    t_hbms, (q_ref, g_ref, c_ref, t_ref, in_sems, out_sems) = refs[:-6], refs[-6:]
    groups = len(t_hbms)
    width = HEADS // groups * DH
    order = list(range(1, groups)) + [0]
    loads = {}
    for k in order:
        cols = pl.ds(pl.multiple_of(group_of(k, groups) * width, DH), width)
        loads[k] = [
            pltpu.make_async_copy(g_hbm.at[:, cols], g_ref.at[k], in_sems.at[0, k]),
            pltpu.make_async_copy(q_hbm.at[:, cols], q_ref.at[k], in_sems.at[1, k]),
        ]
        for copy in loads[k]:
            copy.start()
    coef = coef_of(q_hbm.shape[0])
    stores = []
    for k in order:
        for copy in loads[k]:
            copy.wait()
        for h in range(HEADS // groups):
            cols = pl.ds(h * DH, DH)
            scaled = (g_ref[k, :, cols].astype(F32) * coef).astype(BF16)
            c_ref[k, :, cols] = scaled
            t_ref[k, cols, :] = dot(scaled, q_ref[k, :, cols], TN).astype(BF16)
        cols = pl.ds(pl.multiple_of(group_of(k, groups) * width, DH), width)
        group = [
            pltpu.make_async_copy(t_ref.at[k], t_hbms[k], out_sems.at[0, k]),
            pltpu.make_async_copy(c_ref.at[k], c_hbm.at[:, cols], out_sems.at[1, k]),
        ]
        for copy in group:
            copy.start()
        stores += group
    for copy in stores:
        copy.wait()


def fwd_total_kernel(in_ref, out_ref):
    total = in_ref[0].astype(F32)
    for z in range(1, in_ref.shape[0]):
        total += in_ref[z].astype(F32)
    out_ref[...] = total.astype(BF16)


def fwd_combine_kernel(pair_ref, in_ref, *refs):
    chip_refs, out_ref = refs[:-1], refs[-1]
    span = lax.axis_index("span")
    total = jnp.where(span % 2 == 1, pair_ref[...].astype(F32), 0.0)
    chip = span // 2
    for k in range(len(chip_refs)):
        before = (chip ^ (k + 1)) < chip
        total += jnp.where(before, chip_refs[k][...].astype(F32), 0.0)
    for z in range(in_ref.shape[0]):
        out_ref[z] = total.astype(BF16)
        total += in_ref[z].astype(F32)


def total_kernel(*refs):
    total = refs[0][...].astype(F32)
    for ref in refs[1:-1]:
        total += ref[...].astype(F32)
    refs[-1][...] = total.astype(BF16)


def pair_kernel(a_ref, b_ref, out_ref):
    out_ref[...] = (a_ref[...].astype(F32) + b_ref[...].astype(F32)).astype(BF16)


def back_combine_kernel(groups, pair_ref, *refs):
    chips = len(refs) - 2 * groups - 1
    t_refs, chip_refs = refs[:groups], refs[groups : groups + chips]
    b_refs, held = refs[groups + chips : -1], refs[-1]
    span, plane = lax.axis_index("span"), lax.axis_index("head")
    for k in range(groups):
        held[plane ^ k] = t_refs[k][...]
    total = jnp.where(span % 2 == 0, pair_ref[...].astype(F32), 0.0)
    chip = span // 2
    for k in range(chips):
        after = (chip ^ (k + 1)) > chip
        total += jnp.where(after, chip_refs[k][...].astype(F32), 0.0)
    for z in reversed(range(groups)):
        own = held[z].astype(F32)
        held[z] = total.astype(BF16)
        total += own
    for k in range(groups):
        b_refs[k][...] = held[plane ^ k]


def masked(a, b, mask):
    return jnp.where(mask, dot(a, b, NT), 0.0).astype(BF16)


def square_of(length):
    row = lax.broadcasted_iota(jnp.int32, (length, length), 0)
    return row, lax.broadcasted_iota(jnp.int32, (length, length), 1)


def write(outs, held, sems, slot, first, width):
    cols = pl.ds(pl.multiple_of(first, DH), width)
    copies = [
        pltpu.make_async_copy(held.at[i, slot], out.at[:, cols], sems.at[i, slot])
        for i, out in enumerate(outs)
    ]
    for copy in copies:
        copy.start()
    return copies


def fwd_final_kernel(q_ref, k_ref, v_ref, c_ref, f_ref, out_hbm, dq_hbm, held, sems):
    length = q_ref.shape[0]
    coef = coef_of(length)
    width_in = f_ref.shape[1] // DH
    slots = held.shape[1]
    row, col = square_of(length)
    copies = []
    for slot in range(slots):
        for i in range(HEADS // slots):
            h = slot * (HEADS // slots) + i
            cols, to = pl.ds(h * DH, DH), pl.ds(i * DH, DH)
            q, k, v, c = q_ref[:, cols], k_ref[:, cols], v_ref[:, cols], c_ref[:, cols]
            fwd = f_ref[h // width_in, pl.ds(h % width_in * DH, DH), :]
            own = dot(masked(q, k, col <= row), v) + dot(q, fwd)
            held[0, slot, :, to] = (own * coef).astype(BF16)
            dq = dot(masked(c, v, col <= row), k) + dot(c, fwd, NT)
            held[1, slot, :, to] = dq.astype(BF16)
        width = HEADS // slots * DH
        copies += write((out_hbm, dq_hbm), held, sems, slot, slot * width, width)
    for copy in copies:
        copy.wait()


def back_final_kernel(q_ref, k_ref, v_ref, c_ref, *refs):
    b_refs, (dk_hbm, dv_hbm, held, sems) = refs[:-4], refs[-4:]
    groups = len(b_refs)
    slots = held.shape[1]
    row, col = square_of(q_ref.shape[0])
    copies = []
    for slot in range(slots):
        for i in range(HEADS // slots):
            g = slot * groups // slots
            h = slot * (HEADS // slots) + i - g * (HEADS // groups)
            cols, to = columns(g, groups, h), pl.ds(i * DH, DH)
            q, k, v, c = q_ref[:, cols], k_ref[:, cols], v_ref[:, cols], c_ref[:, cols]
            back = b_refs[g][pl.ds(h * DH, DH), :]
            dk = dot(masked(v, c, col >= row), q) + dot(v, back)
            held[0, slot, :, to] = dk.astype(BF16)
            dv = dot(masked(k, q, col >= row), c) + dot(k, back, NT)
            held[1, slot, :, to] = dv.astype(BF16)
        width = HEADS // slots * DH
        first = group_of(slot, groups) * width if groups > 1 else slot * width
        copies += write((dk_hbm, dv_hbm), held, sems, slot, first, width)
    for copy in copies:
        copy.wait()


def exchange(x, axes="head"):
    return lax.all_to_all(x, axes, split_axis=0, concat_axis=0, tiled=True)


def swap(x, axis, k):
    return lax.ppermute(x, axis, [(i, i ^ k) for i in range(lax.axis_size(axis))])


def over_span(total):
    other = swap(total, "span", 1)
    both = call(pair_kernel, total, 0, total, other)
    chips = range(1, lax.axis_size("span") // 2)
    return other, [swap(both, "span", 2 * k) for k in chips]


def call(kernel, out, flops, *args, scratch=(), ins=None, outs=None, limit=VMEM):
    moved = sum(a.size * a.dtype.itemsize for a in args)
    if not isinstance(out, list):
        out = jax.ShapeDtypeStruct(out.shape, out.dtype)
    vmem = pl.BlockSpec(memory_space=pltpu.VMEM)
    ins = [vmem] * len(args) if ins is None else ins
    if outs is None:
        outs = [vmem] * len(out) if isinstance(out, list) else vmem
    return pl.pallas_call(
        kernel,
        out_shape=out,
        in_specs=ins,
        out_specs=outs,
        scratch_shapes=list(scratch),
        cost_estimate=pl.CostEstimate(flops=flops, bytes_accessed=2 * moved, transcendentals=0),
        compiler_params=pltpu.CompilerParams(vmem_limit_bytes=limit),
    )(*args)


def shards(queries, keys, values, out_grad):
    devices, planes, span = lax.axis_size(AXES), lax.axis_size("head"), lax.axis_size("span")
    length, feat = queries.shape
    share = feat // devices
    direct = direct_on(devices, planes, span)
    groups = planes if direct else 1
    rows_of = jax.ShapeDtypeStruct((length, feat), BF16)
    state_of = jax.ShapeDtypeStruct((groups, feat // groups, DH), BF16)
    piece_of = jax.ShapeDtypeStruct((feat // groups, DH), BF16)
    matmul = 2 * HEADS * length * DH * DH
    hbm = pl.BlockSpec(memory_space=pltpu.HBM)
    vmem = pl.BlockSpec(memory_space=pltpu.VMEM)
    staged = [pltpu.VMEM((groups, length, feat // groups), BF16)] * 3
    staged += [
        pltpu.VMEM((groups, feat // groups, DH), BF16),
        pltpu.SemaphoreType.DMA((2, groups)),
        pltpu.SemaphoreType.DMA((2, groups)),
    ]
    held = [
        pltpu.VMEM((2, 4, length, feat // 4), BF16),
        pltpu.SemaphoreType.DMA((2, 4)),
    ]

    scaled, *back_states = call(
        back_states_kernel, [rows_of] + [piece_of] * groups, matmul,
        queries, out_grad, scratch=staged, ins=[hbm] * 2, outs=[hbm] * (groups + 1), limit=None,
    )
    if direct:
        own = [back_states[0]] + [swap(back_states[k], "head", k) for k in range(1, groups)]
    states = call(fwd_states_kernel, state_of, matmul, keys, values)
    if direct:
        gathered = exchange(states)
        total = call(total_kernel, piece_of, 0, *own)
        other, chips = over_span(total)
        carried = call(
            lambda *refs: back_combine_kernel(groups, *refs),
            [piece_of] * groups, 0, other, *own, *chips,
            scratch=[pltpu.VMEM((groups, feat // groups, DH), BF16)],
        )
        back = [carried[0]] + [swap(carried[k], "head", k) for k in range(1, groups)]
        total = call(fwd_total_kernel, piece_of, 0, gathered)
        other, chips = over_span(total)
        fwd = exchange(call(fwd_combine_kernel, state_of, 0, other, gathered, *chips))
    else:
        wide = exchange(states.reshape(devices, share, DH), AXES).astype(F32)
        before = jnp.cumsum(wide, axis=0) - wide
        fwd = exchange(before.astype(BF16), AXES).reshape(states.shape)
        wide = jnp.flip(exchange(back_states[0].reshape(devices, share, DH), AXES), 0).astype(F32)
        after = jnp.flip(jnp.cumsum(wide, axis=0) - wide, 0)
        back = [exchange(after.astype(BF16), AXES).reshape(feat, DH)]

    rows = (queries, keys, values, scaled)
    out, dq = call(
        fwd_final_kernel, [rows_of] * 2, 6 * matmul, *rows, fwd,
        scratch=held, outs=[hbm] * 2,
    )
    dk, dv = call(
        back_final_kernel, [rows_of] * 2, 6 * matmul, *rows, *back,
        scratch=held, outs=[hbm] * 2,
    )
    return out, dq, dk, dv


def direct_on(devices, planes, span):
    return HEADS * DH // devices % 16 == 0 and planes in (2, 4) and span in (2, 4, 8)


def solution(mesh):
    spec = P(AXES, None)

    return jax.shard_map(
        shards, mesh=mesh, in_specs=(spec,) * 4, out_specs=(spec,) * 4, check_vma=False
    )
```

```python
import jax
import jax.numpy as jnp
from jax import lax
from jax.experimental import pallas as pl
from jax.experimental.pallas import tpu as pltpu
from jax.sharding import PartitionSpec as P


HEADS = 16
DH = 128
F32 = jnp.float32
BF16 = jnp.bfloat16
NT = (((1,), (1,)), ((), ()))
TN = (((0,), (0,)), ((), ()))
AXES = ("span", "head")
VMEM = 20 * 2**20
KEPT = 12
FIRST = ((3,), (2, 1, 0))


def dot(a, b, dims=None):
    if dims is None:
        return jnp.dot(a, b, preferred_element_type=F32)
    return lax.dot_general(a, b, dims, preferred_element_type=F32)


def coef_of(length):
    base = lax.axis_index(AXES) * length
    position = base + lax.broadcasted_iota(jnp.int32, (length, DH), 0)
    return 1.0 / jnp.sqrt(jnp.float32(DH) * (position + 1).astype(F32))


def group_of(k, groups):
    return lax.axis_index("head") ^ k if groups > 1 else 0


def columns(k, groups, h):
    first = (group_of(k, groups) * (HEADS // groups) + h) * DH
    return pl.ds(pl.multiple_of(first, DH), DH)


def fwd_states_kernel(k_ref, v_ref, s_ref):
    parts = DH // s_ref.shape[1]
    for h in range(HEADS):
        cols = pl.ds(h * DH, DH)
        fwd = dot(k_ref[:, cols], v_ref[:, cols], TN).astype(BF16)
        s_ref[pl.ds(h * parts, parts)] = fwd.reshape(parts, DH // parts, DH)


def scaled_of(g, coef):
    return (g.astype(F32) * coef).astype(BF16)


def back_states_kernel(groups, order, q_hbm, g_hbm, *refs):
    t_hbms, (q_ref, g_ref, t_ref, in_sems, out_sems) = refs[:-5], refs[-5:]
    width = HEADS // groups * DH
    loads = []
    for i, k in enumerate(order):
        cols = pl.ds(pl.multiple_of(group_of(k, groups) * width, DH), width)
        loads.append((
            pltpu.make_async_copy(g_hbm.at[:, cols], g_ref.at[i], in_sems.at[0, i]),
            pltpu.make_async_copy(q_hbm.at[:, cols], q_ref.at[i], in_sems.at[1, i]),
        ))
        for copy in loads[-1]:
            copy.start()
    coef = coef_of(q_hbm.shape[0])
    stores = []
    for i in range(len(order)):
        for copy in loads[i]:
            copy.wait()
        for h in range(HEADS // groups):
            cols = pl.ds(h * DH, DH)
            scaled = scaled_of(g_ref[i, :, cols], coef)
            t_ref[i, cols, :] = dot(scaled, q_ref[i, :, cols], TN).astype(BF16)
        stores.append(pltpu.make_async_copy(t_ref.at[i], t_hbms[i], out_sems.at[i]))
        stores[-1].start()
    for copy in stores:
        copy.wait()


def fwd_scan_kernel(in_ref, out_ref):
    def step(i, total):
        out_ref[i] = total.astype(BF16)
        return total + in_ref[i].astype(F32)

    lax.fori_loop(0, in_ref.shape[0], step, jnp.zeros(in_ref.shape[1:], F32), unroll=4)


def total_kernel(*refs):
    t_refs, keep_ref, send_ref = refs[:-2], refs[-2], refs[-1]
    half = keep_ref.shape[0]
    core = lax.axis_index("span") % 2
    for out_ref, part in ((keep_ref, core), (send_ref, 1 - core)):
        rows = pl.ds(pl.multiple_of(part * half, half), half)
        total = t_refs[0][rows, :].astype(F32)
        for ref in t_refs[1:]:
            total += ref[rows, :].astype(F32)
        out_ref[...] = total.astype(BF16)


def pair_kernel(a_ref, b_ref, out_ref):
    out_ref[...] = (a_ref[...].astype(F32) + b_ref[...].astype(F32)).astype(BF16)


def after_kernel(keep_ref, got_ref, *refs):
    chip_refs, own_ref, send_ref = refs[:-2], refs[-2], refs[-1]
    span = lax.axis_index("span")
    chip, first = span // 2, span % 2 == 0
    total = jnp.zeros(own_ref.shape, F32)
    for k, ref in enumerate(chip_refs):
        total += jnp.where((chip ^ (k + 1)) > chip, ref[...].astype(F32), 0.0)
    own_ref[...] = total + jnp.where(first, got_ref[...].astype(F32), 0.0)
    send_ref[...] = (total + jnp.where(first, 0.0, keep_ref[...].astype(F32))).astype(BF16)


def back_combine_kernel(groups, own_ref, other_ref, *refs):
    t_refs, b_refs, held = refs[:groups], refs[groups:-1], refs[-1]
    plane, core = lax.axis_index("head"), lax.axis_index("span") % 2
    half = own_ref.shape[0]
    for k in range(groups):
        held[plane ^ k] = t_refs[k][...]
    for part, ref in ((core, own_ref), (1 - core, other_ref)):
        rows = pl.ds(pl.multiple_of(part * half, half), half)
        total = ref[...].astype(F32)
        for z in reversed(range(groups)):
            own = held[z, rows, :].astype(F32)
            held[z, rows, :] = total.astype(BF16)
            total += own
    for k in range(groups):
        b_refs[k][...] = held[plane ^ k]


def masked(a, b, mask):
    return jnp.where(mask, dot(a, b, NT), 0.0).astype(BF16)


def square_of(length):
    row = lax.broadcasted_iota(jnp.int32, (length, length), 0)
    return row, lax.broadcasted_iota(jnp.int32, (length, length), 1)


def write(outs, held, sems, slot, first, width):
    cols = pl.ds(pl.multiple_of(first, DH), width)
    copies = [
        pltpu.make_async_copy(held.at[i, slot], out.at[:, cols], sems.at[i, slot])
        for i, out in enumerate(outs)
    ]
    for copy in copies:
        copy.start()
    return copies


def fwd_scores_kernel(q_ref, k_ref, v_ref, g_ref, sc_ref, ds_ref):
    coef = coef_of(q_ref.shape[0])
    row, col = square_of(q_ref.shape[0])
    for h in range(HEADS):
        cols = pl.ds(h * DH, DH)
        sc_ref[h] = masked(q_ref[:, cols], k_ref[:, cols], col <= row)
        if h < ds_ref.shape[0]:
            ds_ref[h] = masked(scaled_of(g_ref[:, cols], coef), v_ref[:, cols], col <= row)


def fwd_final_kernel(
    q_ref, k_ref, v_ref, g_ref, sc_ref, ds_ref, f_ref, out_hbm, dq_hbm, held, sems
):
    coef = coef_of(q_ref.shape[0])
    row, col = square_of(q_ref.shape[0])
    parts = DH // f_ref.shape[1]
    slots = held.shape[1]
    copies = []
    for slot in range(slots):
        for i in range(HEADS // slots):
            h = slot * (HEADS // slots) + i
            cols, to = pl.ds(h * DH, DH), pl.ds(i * DH, DH)
            q, k, v = q_ref[:, cols], k_ref[:, cols], v_ref[:, cols]
            c = scaled_of(g_ref[:, cols], coef)
            fwd = f_ref[pl.ds(h * parts, parts)].reshape(DH, DH)
            held[0, slot, :, to] = ((dot(sc_ref[h], v) + dot(q, fwd)) * coef).astype(BF16)
            ds = ds_ref[h] if h < ds_ref.shape[0] else masked(c, v, col <= row)
            held[1, slot, :, to] = (dot(ds, k) + dot(c, fwd, NT)).astype(BF16)
        width = HEADS // slots * DH
        copies += write((out_hbm, dq_hbm), held, sems, slot, slot * width, width)
    for copy in copies:
        copy.wait()


def back_final_kernel(q_ref, k_ref, v_ref, g_ref, *refs):
    b_refs, (dk_hbm, dv_hbm, held, sems) = refs[:-4], refs[-4:]
    groups = len(b_refs)
    slots = held.shape[1]
    coef = coef_of(q_ref.shape[0])
    row, col = square_of(q_ref.shape[0])
    copies = []
    for slot in range(slots):
        for i in range(HEADS // slots):
            g = slot * groups // slots
            h = slot * (HEADS // slots) + i - g * (HEADS // groups)
            cols, to = columns(g, groups, h), pl.ds(i * DH, DH)
            q, k, v = q_ref[:, cols], k_ref[:, cols], v_ref[:, cols]
            c = scaled_of(g_ref[:, cols], coef)
            back = b_refs[g][pl.ds(h * DH, DH), :]
            dk = dot(masked(v, c, col >= row), q) + dot(v, back)
            held[0, slot, :, to] = dk.astype(BF16)
            dv = dot(masked(k, q, col >= row), c) + dot(k, back, NT)
            held[1, slot, :, to] = dv.astype(BF16)
        width = HEADS // slots * DH
        first = group_of(slot, groups) * width if groups > 1 else slot * width
        copies += write((dk_hbm, dv_hbm), held, sems, slot, first, width)
    for copy in copies:
        copy.wait()


def exchange(x):
    return lax.all_to_all(x, AXES, split_axis=0, concat_axis=0, tiled=True)


def swap(x, axis, k):
    return lax.ppermute(x, axis, [(i, i ^ k) for i in range(lax.axis_size(axis))])


def call(kernel, out, flops, *args, scratch=(), ins=None, outs=None, limit=VMEM):
    moved = sum(a.size * a.dtype.itemsize for a in args)
    vmem = pl.BlockSpec(memory_space=pltpu.VMEM)
    ins = [vmem] * len(args) if ins is None else ins
    if outs is None:
        outs = [vmem] * len(out) if isinstance(out, list) else vmem
    return pl.pallas_call(
        kernel,
        out_shape=out,
        in_specs=ins,
        out_specs=outs,
        scratch_shapes=list(scratch),
        cost_estimate=pl.CostEstimate(flops=flops, bytes_accessed=2 * moved, transcendentals=0),
        compiler_params=pltpu.CompilerParams(vmem_limit_bytes=limit),
    )(*args)


def shards(queries, keys, values, out_grad):
    devices, planes, span = lax.axis_size(AXES), lax.axis_size("head"), lax.axis_size("span")
    length, feat = queries.shape
    share = feat // devices
    direct = direct_on(devices, planes, span)
    block = share if direct else DH
    groups = planes if direct else 1
    rows_of = jax.ShapeDtypeStruct((length, feat), BF16)
    state_of = jax.ShapeDtypeStruct((feat // block, block, DH), BF16)
    piece_of = jax.ShapeDtypeStruct((feat // groups, DH), BF16)
    matmul = 2 * HEADS * length * DH * DH
    hbm = pl.BlockSpec(memory_space=pltpu.HBM)
    vmem = pl.BlockSpec(memory_space=pltpu.VMEM)
    held = [
        pltpu.VMEM((2, 4, length, feat // 4), BF16),
        pltpu.SemaphoreType.DMA((2, 4)),
    ]

    back_states = [None] * groups
    for order in FIRST if direct else ((0,),):
        outs = call(
            lambda *refs, order=order: back_states_kernel(groups, order, *refs),
            [piece_of] * len(order), matmul * len(order) // groups,
            queries, out_grad, ins=[hbm] * 2, outs=[hbm] * len(order), limit=None,
            scratch=[
                pltpu.VMEM((len(order), length, feat // groups), BF16),
                pltpu.VMEM((len(order), length, feat // groups), BF16),
                pltpu.VMEM((len(order), feat // groups, DH), BF16),
                pltpu.SemaphoreType.DMA((2, len(order))),
                pltpu.SemaphoreType.DMA((len(order),)),
            ],
        )
        for k, piece in zip(order, outs):
            back_states[k] = piece
    if direct:
        own = [back_states[0]] + [swap(back_states[k], "head", k) for k in range(1, groups)]
    states = call(fwd_states_kernel, state_of, matmul, keys, values)
    if direct:
        gathered = exchange(states)
        fwd = exchange(
            call(fwd_scan_kernel, jax.ShapeDtypeStruct(gathered.shape, BF16), 0, gathered),
        )
        half_of = jax.ShapeDtypeStruct((feat // groups // 2, DH), BF16)
        keep, send = call(total_kernel, [half_of] * 2, 0, *own)
        got = swap(send, "span", 1)
        both = call(pair_kernel, half_of, 0, keep, got)
        chips = [swap(both, "span", 2 * k) for k in range(1, span // 2)]
        wide_of = jax.ShapeDtypeStruct(half_of.shape, F32)
        after, send = call(after_kernel, [wide_of, half_of], 0, keep, got, *chips)
        other = swap(send, "span", 1)
        carried = call(
            lambda *refs: back_combine_kernel(groups, *refs),
            [piece_of] * groups, 0, after, other, *own,
            scratch=[pltpu.VMEM((groups, feat // groups, DH), BF16)],
        )
        back = [carried[0]] + [swap(carried[k], "head", k) for k in range(1, groups)]
    else:
        wide = exchange(states.reshape(devices, share, DH)).astype(F32)
        before = jnp.cumsum(wide, axis=0) - wide
        fwd = exchange(before.astype(BF16)).reshape(states.shape)
        wide = jnp.flip(exchange(back_states[0].reshape(devices, share, DH)), 0).astype(F32)
        after = jnp.flip(jnp.cumsum(wide, axis=0) - wide, 0)
        back = [exchange(after.astype(BF16)).reshape(feat, DH)]

    rows = (queries, keys, values, out_grad)
    scores = call(
        fwd_scores_kernel,
        [jax.ShapeDtypeStruct((heads, length, length), BF16) for heads in (HEADS, KEPT)],
        2 * matmul, *rows,
    )
    out, dq = call(
        fwd_final_kernel, [rows_of] * 2, 4 * matmul, *rows, *scores, fwd,
        scratch=held, outs=[hbm] * 2,
    )
    dk, dv = call(
        back_final_kernel, [rows_of] * 2, 6 * matmul, *rows, *back,
        scratch=held, outs=[hbm] * 2,
    )
    return out, dq, dk, dv


def direct_on(devices, planes, span):
    return HEADS * DH // devices % 16 == 0 and planes == 4 and span in (4, 8)


def solution(mesh):
    spec = P(AXES, None)

    return jax.shard_map(
        shards, mesh=mesh, in_specs=(spec,) * 4, out_specs=(spec,) * 4, check_vma=False
    )
```

```python
import jax
import jax.numpy as jnp
from jax import lax
from jax.experimental import pallas as pl
from jax.experimental.pallas import tpu as pltpu
from jax.sharding import PartitionSpec as P


HEADS = 16
DH = 128
F32 = jnp.float32
BF16 = jnp.bfloat16
NT = (((1,), (1,)), ((), ()))
TN = (((0,), (0,)), ((), ()))
AXES = ("span", "head")
VMEM = 20 * 2**20
KEPT = 12
FIRST = ((3,), (2, 1, 0))


def dot(a, b, dims=None):
    if dims is None:
        return jnp.dot(a, b, preferred_element_type=F32)
    return lax.dot_general(a, b, dims, preferred_element_type=F32)


def joint(a, b, c, d):
    return dot(jnp.concatenate((a, b), 1), jnp.concatenate((c, d), 0))


def coef_of(length):
    base = lax.axis_index(AXES) * length
    position = base + lax.broadcasted_iota(jnp.int32, (length, DH), 0)
    return 1.0 / jnp.sqrt(jnp.float32(DH) * (position + 1).astype(F32))


def group_of(k, groups):
    return lax.axis_index("head") ^ k if groups > 1 else 0


def columns(k, groups, h):
    first = (group_of(k, groups) * (HEADS // groups) + h) * DH
    return pl.ds(pl.multiple_of(first, DH), DH)


def fwd_states_kernel(k_ref, v_ref, s_ref):
    parts = DH // s_ref.shape[1]
    for h in range(HEADS):
        cols = pl.ds(h * DH, DH)
        fwd = dot(k_ref[:, cols], v_ref[:, cols], TN).astype(BF16)
        s_ref[pl.ds(h * parts, parts)] = fwd.reshape(parts, DH // parts, DH)


def scaled_of(g, coef):
    return (g.astype(F32) * coef).astype(BF16)


def back_states_kernel(groups, order, q_hbm, g_hbm, *refs):
    t_hbms, (q_ref, g_ref, t_ref, in_sems, out_sems) = refs[:-5], refs[-5:]
    width = HEADS // groups * DH
    loads = []
    for i, k in enumerate(order):
        cols = pl.ds(pl.multiple_of(group_of(k, groups) * width, DH), width)
        loads.append((
            pltpu.make_async_copy(g_hbm.at[:, cols], g_ref.at[i], in_sems.at[0, i]),
            pltpu.make_async_copy(q_hbm.at[:, cols], q_ref.at[i], in_sems.at[1, i]),
        ))
        for copy in loads[-1]:
            copy.start()
    coef = coef_of(q_hbm.shape[0])
    stores = []
    for i in range(len(order)):
        for copy in loads[i]:
            copy.wait()
        for h in range(HEADS // groups):
            cols = pl.ds(h * DH, DH)
            scaled = scaled_of(g_ref[i, :, cols], coef)
            t_ref[i, cols, :] = dot(scaled, q_ref[i, :, cols], TN).astype(BF16)
        stores.append(pltpu.make_async_copy(t_ref.at[i], t_hbms[i], out_sems.at[i]))
        stores[-1].start()
    for copy in stores:
        copy.wait()


def fwd_scan_kernel(in_ref, out_ref):
    def step(i, total):
        out_ref[i] = total.astype(BF16)
        return total + in_ref[i].astype(F32)

    lax.fori_loop(0, in_ref.shape[0], step, jnp.zeros(in_ref.shape[1:], F32), unroll=4)


def total_kernel(*refs):
    t_refs, keep_ref, send_ref = refs[:-2], refs[-2], refs[-1]
    half = keep_ref.shape[0]
    core = lax.axis_index("span") % 2
    for out_ref, part in ((keep_ref, core), (send_ref, 1 - core)):
        rows = pl.ds(pl.multiple_of(part * half, half), half)
        total = t_refs[0][rows, :].astype(F32)
        for ref in t_refs[1:]:
            total += ref[rows, :].astype(F32)
        out_ref[...] = total.astype(BF16)


def pair_kernel(a_ref, b_ref, out_ref):
    out_ref[...] = (a_ref[...].astype(F32) + b_ref[...].astype(F32)).astype(BF16)


def after_kernel(keep_ref, got_ref, *refs):
    chip_refs, own_ref, send_ref = refs[:-2], refs[-2], refs[-1]
    span = lax.axis_index("span")
    chip, first = span // 2, span % 2 == 0
    total = jnp.zeros(own_ref.shape, F32)
    for k, ref in enumerate(chip_refs):
        total += jnp.where((chip ^ (k + 1)) > chip, ref[...].astype(F32), 0.0)
    own_ref[...] = total + jnp.where(first, got_ref[...].astype(F32), 0.0)
    send_ref[...] = (total + jnp.where(first, 0.0, keep_ref[...].astype(F32))).astype(BF16)


def back_combine_kernel(groups, own_ref, other_ref, *refs):
    t_refs, b_refs, held = refs[:groups], refs[groups:-1], refs[-1]
    plane, core = lax.axis_index("head"), lax.axis_index("span") % 2
    half = own_ref.shape[0]
    for k in range(groups):
        held[plane ^ k] = t_refs[k][...]
    for part, ref in ((core, own_ref), (1 - core, other_ref)):
        rows = pl.ds(pl.multiple_of(part * half, half), half)
        total = ref[...].astype(F32)
        for z in reversed(range(groups)):
            own = held[z, rows, :].astype(F32)
            held[z, rows, :] = total.astype(BF16)
            total += own
    for k in range(groups):
        b_refs[k][...] = held[plane ^ k]


def masked(a, b, mask):
    return jnp.where(mask, dot(a, b, NT), 0.0).astype(BF16)


def square_of(length):
    row = lax.broadcasted_iota(jnp.int32, (length, length), 0)
    return row, lax.broadcasted_iota(jnp.int32, (length, length), 1)


def write(outs, held, sems, slot, first, width):
    cols = pl.ds(pl.multiple_of(first, DH), width)
    copies = [
        pltpu.make_async_copy(held.at[i, slot], out.at[:, cols], sems.at[i, slot])
        for i, out in enumerate(outs)
    ]
    for copy in copies:
        copy.start()
    return copies


def fwd_scores_kernel(q_ref, k_ref, v_ref, g_ref, sc_ref, ds_ref):
    coef = coef_of(q_ref.shape[0])
    row, col = square_of(q_ref.shape[0])
    for h in range(HEADS):
        cols = pl.ds(h * DH, DH)
        sc_ref[h] = masked(q_ref[:, cols], k_ref[:, cols], col <= row)
        if h < ds_ref.shape[0]:
            ds_ref[h] = masked(scaled_of(g_ref[:, cols], coef), v_ref[:, cols], col <= row)


def fwd_final_kernel(
    q_ref, k_ref, v_ref, g_ref, sc_ref, ds_ref, f_ref, out_hbm, dq_hbm, held, sems
):
    coef = coef_of(q_ref.shape[0])
    row, col = square_of(q_ref.shape[0])
    parts = DH // f_ref.shape[1]
    slots = held.shape[1]
    copies = []
    for slot in range(slots):
        for i in range(HEADS // slots):
            h = slot * (HEADS // slots) + i
            cols, to = pl.ds(h * DH, DH), pl.ds(i * DH, DH)
            q, k, v = q_ref[:, cols], k_ref[:, cols], v_ref[:, cols]
            c = scaled_of(g_ref[:, cols], coef)
            fwd = f_ref[pl.ds(h * parts, parts)].reshape(DH, DH)
            out = joint(sc_ref[h], q, v, fwd)
            held[0, slot, :, to] = (out * coef).astype(BF16)
            ds = ds_ref[h] if h < ds_ref.shape[0] else masked(c, v, col <= row)
            held[1, slot, :, to] = (dot(ds, k) + dot(c, fwd, NT)).astype(BF16)
        width = HEADS // slots * DH
        copies += write((out_hbm, dq_hbm), held, sems, slot, slot * width, width)
    for copy in copies:
        copy.wait()


def back_final_kernel(q_ref, k_ref, v_ref, g_ref, *refs):
    b_refs, (dk_hbm, dv_hbm, held, sems) = refs[:-4], refs[-4:]
    groups = len(b_refs)
    slots = held.shape[1]
    coef = coef_of(q_ref.shape[0])
    row, col = square_of(q_ref.shape[0])
    copies = []
    for slot in range(slots):
        for i in range(HEADS // slots):
            g = slot * groups // slots
            h = slot * (HEADS // slots) + i - g * (HEADS // groups)
            cols, to = columns(g, groups, h), pl.ds(i * DH, DH)
            q, k, v = q_ref[:, cols], k_ref[:, cols], v_ref[:, cols]
            c = scaled_of(g_ref[:, cols], coef)
            back = b_refs[g][pl.ds(h * DH, DH), :]
            dk = joint(masked(v, c, col >= row), v, q, back)
            held[0, slot, :, to] = dk.astype(BF16)
            dv = dot(masked(k, q, col >= row), c) + dot(k, back, NT)
            held[1, slot, :, to] = dv.astype(BF16)
        width = HEADS // slots * DH
        first = group_of(slot, groups) * width if groups > 1 else slot * width
        copies += write((dk_hbm, dv_hbm), held, sems, slot, first, width)
    for copy in copies:
        copy.wait()


def exchange(x):
    return lax.all_to_all(x, AXES, split_axis=0, concat_axis=0, tiled=True)


def swap(x, axis, k):
    return lax.ppermute(x, axis, [(i, i ^ k) for i in range(lax.axis_size(axis))])


def call(kernel, out, flops, *args, scratch=(), ins=None, outs=None, limit=VMEM):
    moved = sum(a.size * a.dtype.itemsize for a in args)
    vmem = pl.BlockSpec(memory_space=pltpu.VMEM)
    ins = [vmem] * len(args) if ins is None else ins
    if outs is None:
        outs = [vmem] * len(out) if isinstance(out, list) else vmem
    return pl.pallas_call(
        kernel,
        out_shape=out,
        in_specs=ins,
        out_specs=outs,
        scratch_shapes=list(scratch),
        cost_estimate=pl.CostEstimate(flops=flops, bytes_accessed=2 * moved, transcendentals=0),
        compiler_params=pltpu.CompilerParams(vmem_limit_bytes=limit),
    )(*args)


def shards(queries, keys, values, out_grad):
    devices, planes, span = lax.axis_size(AXES), lax.axis_size("head"), lax.axis_size("span")
    length, feat = queries.shape
    share = feat // devices
    direct = direct_on(devices, planes, span)
    block = share if direct else DH
    groups = planes if direct else 1
    rows_of = jax.ShapeDtypeStruct((length, feat), BF16)
    state_of = jax.ShapeDtypeStruct((feat // block, block, DH), BF16)
    piece_of = jax.ShapeDtypeStruct((feat // groups, DH), BF16)
    matmul = 2 * HEADS * length * DH * DH
    hbm = pl.BlockSpec(memory_space=pltpu.HBM)
    vmem = pl.BlockSpec(memory_space=pltpu.VMEM)
    held = [
        pltpu.VMEM((2, 4, length, feat // 4), BF16),
        pltpu.SemaphoreType.DMA((2, 4)),
    ]

    back_states = [None] * groups
    for order in FIRST if direct else ((0,),):
        outs = call(
            lambda *refs, order=order: back_states_kernel(groups, order, *refs),
            [piece_of] * len(order), matmul * len(order) // groups,
            queries, out_grad, ins=[hbm] * 2, outs=[hbm] * len(order), limit=None,
            scratch=[
                pltpu.VMEM((len(order), length, feat // groups), BF16),
                pltpu.VMEM((len(order), length, feat // groups), BF16),
                pltpu.VMEM((len(order), feat // groups, DH), BF16),
                pltpu.SemaphoreType.DMA((2, len(order))),
                pltpu.SemaphoreType.DMA((len(order),)),
            ],
        )
        for k, piece in zip(order, outs):
            back_states[k] = piece
    if direct:
        own = [back_states[0]] + [swap(back_states[k], "head", k) for k in range(1, groups)]
    states = call(fwd_states_kernel, state_of, matmul, keys, values)
    if direct:
        gathered = exchange(states)
        fwd = exchange(
            call(fwd_scan_kernel, jax.ShapeDtypeStruct(gathered.shape, BF16), 0, gathered),
        )
        half_of = jax.ShapeDtypeStruct((feat // groups // 2, DH), BF16)
        keep, send = call(total_kernel, [half_of] * 2, 0, *own)
        got = swap(send, "span", 1)
        both = call(pair_kernel, half_of, 0, keep, got)
        chips = [swap(both, "span", 2 * k) for k in range(1, span // 2)]
        wide_of = jax.ShapeDtypeStruct(half_of.shape, F32)
        after, send = call(after_kernel, [wide_of, half_of], 0, keep, got, *chips)
        other = swap(send, "span", 1)
        carried = call(
            lambda *refs: back_combine_kernel(groups, *refs),
            [piece_of] * groups, 0, after, other, *own,
            scratch=[pltpu.VMEM((groups, feat // groups, DH), BF16)],
        )
        back = [carried[0]] + [swap(carried[k], "head", k) for k in range(1, groups)]
    else:
        wide = exchange(states.reshape(devices, share, DH)).astype(F32)
        before = jnp.cumsum(wide, axis=0) - wide
        fwd = exchange(before.astype(BF16)).reshape(states.shape)
        wide = jnp.flip(exchange(back_states[0].reshape(devices, share, DH)), 0).astype(F32)
        after = jnp.flip(jnp.cumsum(wide, axis=0) - wide, 0)
        back = [exchange(after.astype(BF16)).reshape(feat, DH)]

    rows = (queries, keys, values, out_grad)
    scores = call(
        fwd_scores_kernel,
        [jax.ShapeDtypeStruct((heads, length, length), BF16) for heads in (HEADS, KEPT)],
        2 * matmul, *rows,
    )
    out, dq = call(
        fwd_final_kernel, [rows_of] * 2, 4 * matmul, *rows, *scores, fwd,
        scratch=held, outs=[hbm] * 2,
    )
    dk, dv = call(
        back_final_kernel, [rows_of] * 2, 6 * matmul, *rows, *back,
        scratch=held, outs=[hbm] * 2,
    )
    return out, dq, dk, dv


def direct_on(devices, planes, span):
    return HEADS * DH // devices % 16 == 0 and planes == 4 and span in (4, 8)


def solution(mesh):
    spec = P(AXES, None)

    return jax.shard_map(
        shards, mesh=mesh, in_specs=(spec,) * 4, out_specs=(spec,) * 4, check_vma=False
    )
```

```python
import jax
import jax.numpy as jnp
from jax import lax
from jax.experimental import pallas as pl
from jax.experimental.pallas import tpu as pltpu
from jax.sharding import PartitionSpec as P


HEADS = 16
DH = 128
F32 = jnp.float32
BF16 = jnp.bfloat16
NT = (((1,), (1,)), ((), ()))
TN = (((0,), (0,)), ((), ()))
AXES = ("span", "head")
VMEM = 20 * 2**20
KEPT = 12
FIRST = ((3, 2), (1, 0))


def dot(a, b, dims=None):
    if dims is None:
        return jnp.dot(a, b, preferred_element_type=F32)
    return lax.dot_general(a, b, dims, preferred_element_type=F32)


def joint(a, b, c, d):
    return dot(jnp.concatenate((a, b), 1), jnp.concatenate((c, d), 0))


def coef_of(length):
    base = lax.axis_index(AXES) * length
    position = base + lax.broadcasted_iota(jnp.int32, (length, DH), 0)
    return 1.0 / jnp.sqrt(jnp.float32(DH) * (position + 1).astype(F32))


def group_of(k, groups):
    return lax.axis_index("head") ^ k if groups > 1 else 0


def columns(k, groups, h):
    first = (group_of(k, groups) * (HEADS // groups) + h) * DH
    return pl.ds(pl.multiple_of(first, DH), DH)


def fwd_states_kernel(k_ref, v_ref, s_ref):
    parts = DH // s_ref.shape[1]
    for h in range(HEADS):
        cols = pl.ds(h * DH, DH)
        fwd = dot(k_ref[:, cols], v_ref[:, cols], TN).astype(BF16)
        s_ref[pl.ds(h * parts, parts)] = fwd.reshape(parts, DH // parts, DH)


def scaled_of(g, coef):
    return (g.astype(F32) * coef).astype(BF16)


def back_states_kernel(groups, order, q_hbm, g_hbm, *refs):
    t_hbms, (q_ref, g_ref, t_ref, in_sems, out_sems) = refs[:-5], refs[-5:]
    width = HEADS // groups * DH
    loads = []
    for i, k in enumerate(order):
        cols = pl.ds(pl.multiple_of(group_of(k, groups) * width, DH), width)
        loads.append((
            pltpu.make_async_copy(g_hbm.at[:, cols], g_ref.at[i], in_sems.at[0, i]),
            pltpu.make_async_copy(q_hbm.at[:, cols], q_ref.at[i], in_sems.at[1, i]),
        ))
        for copy in loads[-1]:
            copy.start()
    coef = coef_of(q_hbm.shape[0])
    stores = []
    for i in range(len(order)):
        for copy in loads[i]:
            copy.wait()
        for h in range(HEADS // groups):
            cols = pl.ds(h * DH, DH)
            scaled = scaled_of(g_ref[i, :, cols], coef)
            t_ref[i, cols, :] = dot(scaled, q_ref[i, :, cols], TN).astype(BF16)
            if h % 2 == 1:
                done = pl.ds((h - 1) * DH, 2 * DH)
                stores.append(
                    pltpu.make_async_copy(
                        t_ref.at[i, done], t_hbms[i].at[done], out_sems.at[i, h // 2]
                    )
                )
                stores[-1].start()
    for copy in stores:
        copy.wait()


def fwd_scan_kernel(in_ref, out_ref):
    def step(i, total):
        out_ref[i] = total.astype(BF16)
        return total + in_ref[i].astype(F32)

    lax.fori_loop(0, in_ref.shape[0], step, jnp.zeros(in_ref.shape[1:], F32), unroll=4)


def total_kernel(*refs):
    t_refs, keep_ref, send_ref = refs[:-2], refs[-2], refs[-1]
    half = keep_ref.shape[0]
    core = lax.axis_index("span") % 2
    for out_ref, part in ((keep_ref, core), (send_ref, 1 - core)):
        rows = pl.ds(pl.multiple_of(part * half, half), half)
        total = t_refs[0][rows, :].astype(F32)
        for ref in t_refs[1:]:
            total += ref[rows, :].astype(F32)
        out_ref[...] = total.astype(BF16)


def pair_kernel(a_ref, b_ref, out_ref):
    out_ref[...] = (a_ref[...].astype(F32) + b_ref[...].astype(F32)).astype(BF16)


def after_kernel(keep_ref, got_ref, *refs):
    chip_refs, own_ref, send_ref = refs[:-2], refs[-2], refs[-1]
    span = lax.axis_index("span")
    chip, first = span // 2, span % 2 == 0
    total = jnp.zeros(own_ref.shape, F32)
    for k, ref in enumerate(chip_refs):
        total += jnp.where((chip ^ (k + 1)) > chip, ref[...].astype(F32), 0.0)
    own_ref[...] = total + jnp.where(first, got_ref[...].astype(F32), 0.0)
    send_ref[...] = (total + jnp.where(first, 0.0, keep_ref[...].astype(F32))).astype(BF16)


def back_combine_kernel(groups, own_ref, other_ref, *refs):
    t_refs, b_refs, held = refs[:groups], refs[groups:-1], refs[-1]
    plane, core = lax.axis_index("head"), lax.axis_index("span") % 2
    half = own_ref.shape[0]
    for k in range(groups):
        held[plane ^ k] = t_refs[k][...]
    for part, ref in ((core, own_ref), (1 - core, other_ref)):
        rows = pl.ds(pl.multiple_of(part * half, half), half)
        total = ref[...].astype(F32)
        for z in reversed(range(groups)):
            own = held[z, rows, :].astype(F32)
            held[z, rows, :] = total.astype(BF16)
            total += own
    for k in range(groups):
        b_refs[k][...] = held[plane ^ k]


def masked(a, b, mask):
    return jnp.where(mask, dot(a, b, NT), 0.0).astype(BF16)


def square_of(length):
    row = lax.broadcasted_iota(jnp.int32, (length, length), 0)
    return row, lax.broadcasted_iota(jnp.int32, (length, length), 1)


def write(outs, held, sems, slot, first, width):
    cols = pl.ds(pl.multiple_of(first, DH), width)
    copies = [
        pltpu.make_async_copy(held.at[i, slot], out.at[:, cols], sems.at[i, slot])
        for i, out in enumerate(outs)
    ]
    for copy in copies:
        copy.start()
    return copies


def fwd_scores_kernel(q_ref, k_ref, v_ref, g_ref, sc_ref, ds_ref):
    coef = coef_of(q_ref.shape[0])
    row, col = square_of(q_ref.shape[0])
    for h in range(HEADS):
        cols = pl.ds(h * DH, DH)
        sc_ref[h] = masked(q_ref[:, cols], k_ref[:, cols], col <= row)
        if h < ds_ref.shape[0]:
            ds_ref[h] = masked(scaled_of(g_ref[:, cols], coef), v_ref[:, cols], col <= row)


def fwd_final_kernel(
    q_ref, k_ref, v_ref, g_ref, sc_ref, ds_ref, f_ref, out_hbm, dq_hbm, held, sems
):
    coef = coef_of(q_ref.shape[0])
    row, col = square_of(q_ref.shape[0])
    parts = DH // f_ref.shape[1]
    slots = held.shape[1]
    copies = []
    for slot in range(slots):
        for i in range(HEADS // slots):
            h = slot * (HEADS // slots) + i
            cols, to = pl.ds(h * DH, DH), pl.ds(i * DH, DH)
            q, k, v = q_ref[:, cols], k_ref[:, cols], v_ref[:, cols]
            c = scaled_of(g_ref[:, cols], coef)
            fwd = f_ref[pl.ds(h * parts, parts)].reshape(DH, DH)
            out = joint(sc_ref[h], q, v, fwd)
            held[0, slot, :, to] = (out * coef).astype(BF16)
            ds = ds_ref[h] if h < ds_ref.shape[0] else masked(c, v, col <= row)
            held[1, slot, :, to] = (dot(ds, k) + dot(c, fwd, NT)).astype(BF16)
        width = HEADS // slots * DH
        copies += write((out_hbm, dq_hbm), held, sems, slot, slot * width, width)
    for copy in copies:
        copy.wait()


def back_final_kernel(q_ref, k_ref, v_ref, g_ref, *refs):
    b_refs, (dk_hbm, dv_hbm, held, sems) = refs[:-4], refs[-4:]
    groups = len(b_refs)
    slots = held.shape[1]
    coef = coef_of(q_ref.shape[0])
    row, col = square_of(q_ref.shape[0])
    copies = []
    for slot in range(slots):
        for i in range(HEADS // slots):
            g = slot * groups // slots
            h = slot * (HEADS // slots) + i - g * (HEADS // groups)
            cols, to = columns(g, groups, h), pl.ds(i * DH, DH)
            q, k, v = q_ref[:, cols], k_ref[:, cols], v_ref[:, cols]
            c = scaled_of(g_ref[:, cols], coef)
            back = b_refs[g][pl.ds(h * DH, DH), :]
            dk = joint(masked(v, c, col >= row), v, q, back)
            held[0, slot, :, to] = dk.astype(BF16)
            dv = dot(masked(k, q, col >= row), c) + dot(k, back, NT)
            held[1, slot, :, to] = dv.astype(BF16)
        width = HEADS // slots * DH
        first = group_of(slot, groups) * width if groups > 1 else slot * width
        copies += write((dk_hbm, dv_hbm), held, sems, slot, first, width)
    for copy in copies:
        copy.wait()


def exchange(x):
    return lax.all_to_all(x, AXES, split_axis=0, concat_axis=0, tiled=True)


def swap(x, axis, k):
    return lax.ppermute(x, axis, [(i, i ^ k) for i in range(lax.axis_size(axis))])


def call(kernel, out, flops, *args, scratch=(), ins=None, outs=None, limit=VMEM):
    moved = sum(a.size * a.dtype.itemsize for a in args)
    vmem = pl.BlockSpec(memory_space=pltpu.VMEM)
    ins = [vmem] * len(args) if ins is None else ins
    if outs is None:
        outs = [vmem] * len(out) if isinstance(out, list) else vmem
    return pl.pallas_call(
        kernel,
        out_shape=out,
        in_specs=ins,
        out_specs=outs,
        scratch_shapes=list(scratch),
        cost_estimate=pl.CostEstimate(flops=flops, bytes_accessed=2 * moved, transcendentals=0),
        compiler_params=pltpu.CompilerParams(vmem_limit_bytes=limit),
    )(*args)


def shards(queries, keys, values, out_grad):
    devices, planes, span = lax.axis_size(AXES), lax.axis_size("head"), lax.axis_size("span")
    length, feat = queries.shape
    share = feat // devices
    direct = direct_on(devices, planes, span)
    block = share if direct else DH
    groups = planes if direct else 1
    rows_of = jax.ShapeDtypeStruct((length, feat), BF16)
    state_of = jax.ShapeDtypeStruct((feat // block, block, DH), BF16)
    piece_of = jax.ShapeDtypeStruct((feat // groups, DH), BF16)
    matmul = 2 * HEADS * length * DH * DH
    hbm = pl.BlockSpec(memory_space=pltpu.HBM)
    vmem = pl.BlockSpec(memory_space=pltpu.VMEM)
    held = [
        pltpu.VMEM((2, 4, length, feat // 4), BF16),
        pltpu.SemaphoreType.DMA((2, 4)),
    ]

    back_states = [None] * groups
    for order in FIRST if direct else ((0,),):
        outs = call(
            lambda *refs, order=order: back_states_kernel(groups, order, *refs),
            [piece_of] * len(order), matmul * len(order) // groups,
            queries, out_grad, ins=[hbm] * 2, outs=[hbm] * len(order), limit=None,
            scratch=[
                pltpu.VMEM((len(order), length, feat // groups), BF16),
                pltpu.VMEM((len(order), length, feat // groups), BF16),
                pltpu.VMEM((len(order), feat // groups, DH), BF16),
                pltpu.SemaphoreType.DMA((2, len(order))),
                pltpu.SemaphoreType.DMA((len(order), HEADS // groups // 2)),
            ],
        )
        for k, piece in zip(order, outs):
            back_states[k] = piece
    if direct:
        own = [back_states[0]] + [swap(back_states[k], "head", k) for k in range(1, groups)]
    states = call(fwd_states_kernel, state_of, matmul, keys, values)
    if direct:
        gathered = exchange(states)
        fwd = exchange(
            call(fwd_scan_kernel, jax.ShapeDtypeStruct(gathered.shape, BF16), 0, gathered),
        )
        half_of = jax.ShapeDtypeStruct((feat // groups // 2, DH), BF16)
        keep, send = call(total_kernel, [half_of] * 2, 0, *own)
        got = swap(send, "span", 1)
        both = call(pair_kernel, half_of, 0, keep, got)
        chips = [swap(both, "span", 2 * k) for k in range(1, span // 2)]
        wide_of = jax.ShapeDtypeStruct(half_of.shape, F32)
        after, send = call(after_kernel, [wide_of, half_of], 0, keep, got, *chips)
        other = swap(send, "span", 1)
        carried = call(
            lambda *refs: back_combine_kernel(groups, *refs),
            [piece_of] * groups, 0, after, other, *own,
            scratch=[pltpu.VMEM((groups, feat // groups, DH), BF16)],
        )
        back = [carried[0]] + [swap(carried[k], "head", k) for k in range(1, groups)]
    else:
        wide = exchange(states.reshape(devices, share, DH)).astype(F32)
        before = jnp.cumsum(wide, axis=0) - wide
        fwd = exchange(before.astype(BF16)).reshape(states.shape)
        wide = jnp.flip(exchange(back_states[0].reshape(devices, share, DH)), 0).astype(F32)
        after = jnp.flip(jnp.cumsum(wide, axis=0) - wide, 0)
        back = [exchange(after.astype(BF16)).reshape(feat, DH)]

    rows = (queries, keys, values, out_grad)
    scores = call(
        fwd_scores_kernel,
        [jax.ShapeDtypeStruct((heads, length, length), BF16) for heads in (HEADS, KEPT)],
        2 * matmul, *rows,
    )
    out, dq = call(
        fwd_final_kernel, [rows_of] * 2, 4 * matmul, *rows, *scores, fwd,
        scratch=held, outs=[hbm] * 2,
    )
    dk, dv = call(
        back_final_kernel, [rows_of] * 2, 6 * matmul, *rows, *back,
        scratch=held, outs=[hbm] * 2,
    )
    return out, dq, dk, dv


def direct_on(devices, planes, span):
    return HEADS * DH // devices % 16 == 0 and planes == 4 and span in (4, 8)


def solution(mesh):
    spec = P(AXES, None)

    return jax.shard_map(
        shards, mesh=mesh, in_specs=(spec,) * 4, out_specs=(spec,) * 4, check_vma=False
    )
```
